32 devices in a mesh: group: 2 (over y), scen: 4 (over z), inst: 2 (over x), acct: 2 (over core).
Axes of the slice: x: 2, y: 2, z: 4, core: 2. Of those that a mesh axis runs over, the one named last changes fastest.
Arguments:
- returns: float32 [4096, 1024], P(('group', 'scen')), parts along dimension 0, may hold values from -40 to 40, as said below
- prior: float32 [18, 1024], P('group'), parts along dimension 0, may hold values from -15 to 15
- decay: float32 [1024], replicated, may hold values from 0.000146484375 to 0.06
- seed_var: float32 [1024], replicated, may hold values from 0.2 to 8
- date_offsets: int32 [2048], P('scen'), may hold values from 0 to 2
- block_index: int32 [32768], P(('group', 'inst', 'acct')), parts along dimension 0, may hold values from 0 to 7
- delta_sens: bfloat16 [128, 32768], P(None, ('group', 'inst', 'acct')), parts along dimension 1, may hold values from -0.0625 to 0.0625
- gamma_sens: bfloat16 [128, 32768], P(None, ('group', 'inst', 'acct')), parts along dimension 1, may hold values from -0.0046691895 to 0.0046691895
- positions: bfloat16 [256, 16384], P('group', ('inst', 'acct')), parts along dimension 0, may hold values from -0.09375 to 0.09375
- pattern: int32 [256, 128], P('group', ('inst', 'acct')), parts along dimension 0, may hold values 0 or 1
Outputs:
- acct_pnl: float32 [256, 2048], P(('group', 'scen', 'inst', 'acct')), parts along dimension 0
- margin: float32 [256], P(('group', 'scen', 'inst', 'acct')), parts along dimension 0
The draws below stay inside these ranges and needn't reach their ends.
There are 2 independent parts, one for each index of `group`. The reference program is written for one: setup_inputs(seed, part) draws one part's arguments, and reference() takes and returns one part's arrays. A program takes and returns all parts, laid end to end along the dimension named above; an argument that names none is the same for every part. Nothing has to cross between parts.
Inputs may be any that keep to these rules, and one draw needn't show every extreme that they name: Fat tailed daily returns.
All inputs are finite; a program needn't handle non-finite values. No bound on the sum of `pattern` on one device may be relied on, other than what follows from the above.
Results may differ from the reference program's by a relative error of at most 0.004.
Values sent between devices are 32-bit elements; how exact they have to be, the bound alone decides.
A program may use at most 128 MiB of HBM per device.

```python
import math
import jax
import jax.numpy as jnp
from jax import lax

F = 1024
BW = 128
PB = 128
WIN = 10
NBLK = 8
SCEN = 2048
INSTR = 16384
ACCT = 128
TAIL = 51


def draw_returns(key, part):
    noise_key, day_key, factor_key = jax.random.split(jax.random.fold_in(key, 11), 3)
    noise_draw = jax.random.normal(noise_key, (SCEN, F), jnp.float32)
    day_scale = jnp.exp(jax.random.uniform(day_key, (SCEN, 1), jnp.float32, math.log(0.3), math.log(3.0)))
    factor_scale = jnp.exp(jax.random.uniform(factor_key, (1, F), jnp.float32, math.log(0.3), math.log(3.0)))
    return jnp.clip(noise_draw * day_scale * factor_scale, -40.0, 40.0)


def draw_decay(key, part):
    pick_key, rate_key = jax.random.split(jax.random.fold_in(key, 23), 2)
    slow_share = 0.5
    spread_draw = jax.random.uniform(rate_key, (F,), jnp.float32)
    slow_rate = (0.3 + 1.7 * spread_draw) / SCEN
    fast_rate = 0.02 + 0.04 * spread_draw
    picked = jax.random.uniform(pick_key, (F,), jnp.float32) < slow_share
    return jnp.where(picked, slow_rate, fast_rate)


def place_ends(array, stream_key, least, high):
    longest = array.shape.index(max(array.shape))
    spots = []
    for shift in (0, 1):
        where = [jax.random.randint(jax.random.fold_in(stream_key, axis), (), 0, length) for axis, length in enumerate(array.shape)]
        where[longest] = (where[longest] + shift) % array.shape[longest]
        spots.append(tuple(where))
    return array.at[spots[0]].set(least).at[spots[1]].set(high)


def block_scale(stream_key, extent, cuts, low, high):
    gain, own = 1.0, jax.random.fold_in(stream_key, 6)
    for position, shards_of in cuts:
        draws = jnp.exp(jax.random.uniform(jax.random.fold_in(own, position), (shards_of,), jnp.float32, low / len(cuts), high / len(cuts)))
        gain = gain * jnp.repeat(draws, extent[position] // shards_of).reshape([-1 if axis == position else 1 for axis in range(len(extent))])
    return gain


def normal_values(own_key, extent, scale, reach, pieces=(), kind=jnp.bfloat16):
    result = jax.random.normal(own_key, extent, jnp.float32) * scale
    if len(pieces) > 0:
        result = block_scale(own_key, extent, pieces, -0.22, 0.18) * result
    return jnp.clip(result, min=-reach, max=reach).astype(kind)


def setup_inputs(seed: int = 0, part: int = 0) -> dict:
    key_list = jax.random.split(jax.random.key(seed), 11)
    part_splits = jax.random.split(jax.random.fold_in(key_list[10], part), 11)
    returns = draw_returns(jax.random.fold_in(jax.random.fold_in(key_list[10], part), 71), part)
    prior = normal_values(part_splits[1], (WIN - 1, F), 3.0, 15.0, (), jnp.float32)
    decay = draw_decay(jax.random.fold_in(key_list[10], 71), part)
    seed_var = jnp.clip(jnp.exp(jax.random.uniform(key_list[3], (F,), jnp.float32, math.log(0.2), math.log(8.0))), 0.2, 8.0)
    date_offsets = place_ends(jax.random.randint(key_list[4], (SCEN,), 0, 3), jax.random.fold_in(key_list[4], 1), 0, 2).astype(jnp.int32)
    block_index = place_ends(jax.random.randint(part_splits[5], (INSTR,), 0, NBLK), jax.random.fold_in(part_splits[5], 1), 0, NBLK - 1).astype(jnp.int32)
    delta_sens = normal_values(part_splits[6], (BW, INSTR), (64 * BW) ** -0.5, 0.0625, ((1, 4),))
    gamma_sens = normal_values(part_splits[7], (BW, INSTR), (0.1 / BW), 0.0046691895, ((1, 4),))
    positions = normal_values(part_splits[8], (ACCT, INSTR), (INSTR // 4) ** -0.5, 0.09375, ((1, 4),))
    pattern = place_ends((jax.random.randint(part_splits[9], (ACCT, INSTR // PB), 0, 4) < 1).astype(jnp.int32), jax.random.fold_in(part_splits[9], 1), 0, 1)
    return {"returns": returns, "prior": prior, "decay": decay, "seed_var": seed_var, "date_offsets": date_offsets, "block_index": block_index, "delta_sens": delta_sens, "gamma_sens": gamma_sens, "positions": positions, "pattern": pattern}


def window_sum(extended, date_offsets, row_count):
    window_total = jnp.zeros((row_count, extended.shape[1]), jnp.float32)
    for lag_step in range(WIN):
        keep_mask = (date_offsets <= lag_step)[:, None]
        window_total = window_total + jnp.where(keep_mask, extended[lag_step:lag_step + row_count], 0.0)
    return window_total

def reference(returns, prior, decay, seed_var, date_offsets, block_index, delta_sens, gamma_sens, positions, pattern):
    retain = 1.0 - decay

    def advance(carried, day_return):
        carried = retain * carried + decay * day_return * day_return
        return (carried, carried)
    _, variance = lax.scan(advance, seed_var, returns)
    scaled = returns * jnp.sqrt(variance[-1] / variance)
    extended = jnp.concatenate([prior, scaled], axis=0)
    scen_moves = window_sum(extended, date_offsets, SCEN)
    features = jnp.concatenate([scen_moves.astype(jnp.bfloat16), (0.5 * scen_moves * scen_moves).astype(jnp.bfloat16)], axis=1)
    chosen = block_index[None, :] == jnp.arange(NBLK, dtype=jnp.int32)[:, None]
    dense_delta = jnp.where(chosen[:, None, :], delta_sens[None], 0).astype(jnp.bfloat16).reshape(F, INSTR)
    dense_gamma = jnp.where(chosen[:, None, :], gamma_sens[None], 0).astype(jnp.bfloat16).reshape(F, INSTR)
    sensitivity = jnp.concatenate([dense_delta, dense_gamma], axis=0)
    inst_pnl = jnp.dot(features, sensitivity, preferred_element_type=jnp.float32).astype(jnp.bfloat16)
    held_pos = jnp.where(pattern[:, :, None] > 0, positions.reshape(ACCT, INSTR // PB, PB), 0).astype(jnp.bfloat16).reshape(ACCT, INSTR)
    acct_pnl = lax.dot_general(held_pos, inst_pnl, (((1,), (1,)), ((), ())), preferred_element_type=jnp.float32)
    losses = lax.top_k(-acct_pnl, TAIL)[0]
    margin = lax.optimization_barrier(jnp.mean(losses, axis=1))
    return (acct_pnl, margin)
```

```python
import functools

import jax
import jax.numpy as jnp
from jax import lax
from jax.experimental import pallas as pl
from jax.experimental.pallas import tpu as pltpu
from jax.sharding import PartitionSpec as P

WIN = 10
LANES = 128
SUB = 8
MESH = pl.DeviceIdType.MESH
NT = (((1,), (1,)), ((), ()))


def ipow(x, n):
    result = None
    while n:
        if n & 1:
            result = x if result is None else result * x
        n >>= 1
        if n:
            x = x * x
    return result


def kernel(
    sizes,
    ret_h, prior_h, dec_h, seed_h, off_h, bidx_h, delta_h, gamma_h, pos_h, pat_h,
    out_ref, marg_ref,
    ret, prior, dec, seed, off, bidx, sens, pos, pat,
    offb, state, start, ends, tail_out, tail_in, moves, wacc, whl, fcat,
    part, rs_in, summ, fin,
    in_sem, ret_sem, end_ss, end_rs, tail_ss, tail_rs, rs_ss, rs_rs, fin_ss, fin_rs,
):
    S, I, A, T = sizes
    owners = I * A
    rank = lax.axis_index("scen")
    inst, acct = lax.axis_index("inst"), lax.axis_index("acct")
    me = inst * A + acct
    C, R, _ = ret.shape
    L = R // SUB
    H = WIN - 1
    BW = delta_h.shape[0]
    accts, instr = pos.shape
    AL = accts // (S * owners)
    f32, bf16 = jnp.float32, jnp.bfloat16

    small = [
        pltpu.make_async_copy(src, dst, in_sem.at[n])
        for n, (src, dst) in enumerate(
            [(off_h, off), (dec_h, dec), (seed_h, seed), (prior_h, prior)]
        )
    ]
    late = [
        pltpu.make_async_copy(src, dst, in_sem.at[4 + n])
        for n, (src, dst) in enumerate(
            [
                (bidx_h, bidx),
                (pat_h, pat),
                (delta_h, sens.at[pl.ds(0, BW)]),
                (gamma_h, sens.at[pl.ds(BW, BW)]),
                (pos_h, pos),
            ]
        )
    ]
    cols = [
        pltpu.make_async_copy(
            ret_h.at[:, pl.ds(c * LANES, LANES)], ret.at[c], ret_sem.at[c]
        )
        for c in range(C)
    ]
    for copy in small + cols + late:
        copy.start()

    def owner_id(d):
        who = lax.rem(me + d, owners)
        return {"inst": who // A, "acct": lax.rem(who, A)}

    barrier = pltpu.get_barrier_semaphore()
    for d in range(1, S):
        pl.semaphore_signal(
            barrier, inc=1, device_id={"scen": lax.rem(rank + d, S)}, device_id_type=MESH
        )
    for d in range(1, owners):
        pl.semaphore_signal(barrier, inc=1, device_id=owner_id(d), device_id_type=MESH)

    for copy in small:
        copy.wait()
    row = lax.broadcasted_iota(jnp.int32, (R, R), 0)
    day = lax.broadcasted_iota(jnp.int32, (R, R), 1)
    pick = jnp.where((row % SUB) * L + row // SUB == day, 1.0, 0.0).astype(bf16)
    spread = jnp.broadcast_to(off[...].astype(f32), (LANES, R)).astype(bf16)
    offb[...] = lax.dot_general(pick, spread, NT, preferred_element_type=f32).reshape(
        L, SUB, LANES
    )

    keep_rows = 1.0 - dec[...]
    dec_c = [jnp.broadcast_to(dec[c : c + 1, :], (SUB, LANES)) for c in range(C)]
    keep_c = [1.0 - dec_c[c] for c in range(C)]
    for copy in cols:
        copy.wait()

    def scan(t, carry):
        new = []
        for c in range(C):
            x = ret[c, pl.ds(t, SUB, stride=L), :]
            v = keep_c[c] * carry[c] + dec_c[c] * x * x
            state[t, c] = v
            new.append(v)
        return tuple(new)

    zero = jnp.zeros((SUB, LANES), f32)
    last = lax.fori_loop(0, L, scan, (zero,) * C, unroll=4)

    sub = lax.broadcasted_iota(jnp.int32, (SUB, LANES), 0)
    for c in range(C):
        run = ipow(keep_c[c], L)
        x = last[c]
        for hop in (1, 2, 4):
            x = x + jnp.where(sub >= hop, run * pltpu.roll(x, hop, 0), 0.0)
            run = run * run
        ends[rank, c : c + 1, :] = x[SUB - 1 :, :]
        before = jnp.where(sub >= 1, pltpu.roll(x, 1, 0), 0.0)
        start[c] = before
        z = ipow(keep_c[c], L - H) * before
        for n in range(H):
            z = z * keep_c[c]
            v = state[L - H + n, c] + z
            tail_out[n, c : c + 1, :] = ret[c, R - H + n : R - H + n + 1, :]
            tail_out[H + n, c : c + 1, :] = v[SUB - 1 :, :]

    pl.semaphore_wait(barrier, S - 1 + owners - 1)
    sends = []
    for d in range(1, S):
        sends.append(
            pltpu.make_async_remote_copy(
                src_ref=ends.at[rank],
                dst_ref=ends.at[rank],
                send_sem=end_ss.at[d],
                recv_sem=end_rs.at[d],
                device_id={"scen": lax.rem(rank + d, S)},
                device_id_type=MESH,
            )
        )
    sends.append(
        pltpu.make_async_remote_copy(
            src_ref=tail_out,
            dst_ref=tail_in,
            send_sem=tail_ss,
            recv_sem=tail_rs,
            device_id={"scen": lax.rem(rank + 1, S)},
            device_id_type=MESH,
        )
    )
    for copy in sends:
        copy.start()

    for copy in late:
        copy.wait()
    AT = min(accts, 128)
    CH = min(instr, 512)
    blocks = pat.shape[1]
    PB = instr // blocks

    wacc[...] = jnp.zeros_like(wacc)

    def weigh(step, _):
        q, at = step // (accts // AT), lax.rem(step, accts // AT)
        rows = pl.ds(pl.multiple_of(at * AT, AT), AT)
        at_cols = pl.ds(pl.multiple_of(q * CH, CH), CH)
        ahead = lax.broadcasted_iota(jnp.int32, (blocks, CH), 1) + q * CH
        which = lax.broadcasted_iota(jnp.int32, (blocks, CH), 0) * PB
        widen = jnp.where((ahead >= which) & (ahead < which + PB), 1.0, 0.0).astype(bf16)
        holds = jnp.where(pat[rows, :] > 0, 1.0, 0.0).astype(bf16)
        mask = jnp.dot(holds, widen, preferred_element_type=f32).astype(bf16)
        held = pos[rows, at_cols] * mask
        own = bidx[:, at_cols]
        parts = [
            held * jnp.broadcast_to(jnp.where(own == b, 1.0, 0.0), (AT, CH)).astype(bf16)
            for b in range(C)
        ]
        got = lax.dot_general(
            jnp.concatenate(parts, axis=0), sens[:, at_cols], NT, preferred_element_type=f32
        )
        wacc[:, rows, :] += got.reshape(C, AT, 2 * BW)
        return 0

    lax.fori_loop(0, (instr // CH) * (accts // AT), weigh, 0)

    def split(step, _):
        c, at = step // (accts // AT), lax.rem(step, accts // AT)
        w = wacc[c, pl.ds(pl.multiple_of(at * AT, AT), AT), :]
        high = w.astype(bf16)
        whl[at, c, :AT, :] = high
        whl[at, c, AT:, :] = (w - high.astype(f32)).astype(bf16)
        return 0

    lax.fori_loop(0, C * (accts // AT), split, 0)

    for copy in sends:
        copy.wait()

    span = ipow(keep_rows, R)
    var = seed[...]
    entering = var
    entering_prev = var
    for n in range(S):
        entering = jnp.where(rank == n, var, entering)
        entering_prev = jnp.where(rank == n + 1, var, entering_prev)
        var = span * var + ends[n]
    root = jnp.sqrt(var)

    power = ipow(keep_rows, R - H)
    lead = []
    for n in range(H):
        power = power * keep_rows
        lead.append(
            tail_in[n] * (root * lax.rsqrt(tail_in[H + n] + power * entering_prev))
        )

    root_c, z0, heads = [], [], [[] for _ in range(C)]
    for c in range(C):
        root_b = jnp.broadcast_to(root[c : c + 1, :], (SUB, LANES))
        enter_b = jnp.broadcast_to(entering[c : c + 1, :], (SUB, LANES))
        run = ipow(keep_c[c], L)
        run_pow = jnp.ones((SUB, LANES), f32)
        for j in range(1, SUB):
            run_pow = jnp.where(sub >= j, run_pow * run, run_pow)
        z = start[c] + run_pow * enter_b
        root_c.append(root_b)
        z0.append(z)
        z = z * ipow(keep_c[c], L - H)
        for n in range(H):
            z = z * keep_c[c]
            t = L - H + n
            x = ret[c, pl.ds(t, SUB, stride=L), :]
            e = x * (root_b * lax.rsqrt(state[t, c] + z))
            first = jnp.where(
                rank == 0,
                prior[n : n + 1, c * LANES : (c + 1) * LANES],
                lead[n][c : c + 1, :],
            )
            heads[c].append(
                jnp.where(sub == 0, jnp.broadcast_to(first, (SUB, LANES)), pltpu.roll(e, 1, 0))
            )

    G, PAIR = 8, 2

    def window(group, block, carry):
        t0 = block * G
        new = []
        offs = [offb[t0 + i] for i in range(G)]
        for c, (z, e) in zip(group, carry):
            e = list(e)
            for i in range(G):
                z = z * keep_c[c]
                x = ret[c, pl.ds(t0 + i, SUB, stride=L), :]
                e.append(x * (root_c[c] * lax.rsqrt(state[t0 + i, c] + z)))
            new.append((z, tuple(e[G:])))
            two = {i: e[i] + e[i - 1] for i in range(3, G + H)}
            four = {i: two[i] + two[i - 2] for i in range(5, G + H)}
            for i in range(G):
                p = i + H
                total = four[p] + four[p - 4]
                total = total + jnp.where(offs[i] < 1.5, e[p - 8], 0.0)
                total = total + jnp.where(offs[i] < 0.5, e[p - 9], 0.0)
                moves[c, pl.ds(t0 + i, SUB, stride=L), :] = total
        return tuple(new)

    for g in range(0, C, PAIR):
        group = tuple(range(g, min(g + PAIR, C)))
        lax.fori_loop(
            0, L // G, functools.partial(window, group), tuple((z0[c], tuple(heads[c])) for c in group)
        )

    for c in range(C):
        m = moves[c]
        fcat[c, :, :LANES] = m.astype(bf16)
        fcat[c, :, LANES:] = (0.5 * m * m).astype(bf16)

    per = AT // AL

    def combine(at, _):
        both = jnp.zeros((2 * AT, R), f32)
        for c in range(C):
            both = both + lax.dot_general(
                whl[at, c], fcat[c], NT, preferred_element_type=f32
            )
        total = both[:AT] + both[AT:]
        for i in range(per):
            part[i % owners, at * (per // owners) + i // owners] = total[i * AL : (i + 1) * AL]
        return 0

    lax.fori_loop(0, accts // AT, combine, 0)

    hops = []
    for d in range(1, owners):
        hops.append(
            pltpu.make_async_remote_copy(
                src_ref=part.at[lax.rem(me + d, owners)],
                dst_ref=rs_in.at[d - 1],
                send_sem=rs_ss.at[d],
                recv_sem=rs_rs.at[d],
                device_id=owner_id(d),
                device_id_type=MESH,
            )
        )
    for copy in hops:
        copy.start()
    for copy in hops:
        copy.wait()
    for k in range(S):
        total = part[me, k]
        for d in range(1, owners):
            total = total + rs_in[d - 1, k]
        summ[k] = total

    outs = []
    for d in range(1, S):
        to = lax.rem(rank + d, S)
        outs.append(
            pltpu.make_async_remote_copy(
                src_ref=summ.at[to],
                dst_ref=fin.at[rank],
                send_sem=fin_ss.at[d],
                recv_sem=fin_rs.at[d],
                device_id={"scen": to},
                device_id_type=MESH,
            )
        )
    for copy in outs:
        copy.start()
    fin[rank] = summ[rank]
    for copy in outs:
        copy.wait()

    xs = []
    for k in range(S):
        y = fin[k]
        out_ref[:, k * R : (k + 1) * R] = y
        xs.extend(-y[:, i * LANES : (i + 1) * LANES] for i in range(R // LANES))

    groups = -(-T // LANES)
    each = len(xs) // groups
    peaks = []
    for g in range(groups):
        mine = xs[g * each : (g + 1) * each] if g < groups - 1 else xs[g * each :]
        peaks.append(functools.reduce(jnp.maximum, mine))
    high = jnp.max(functools.reduce(jnp.maximum, peaks), axis=1, keepdims=True)
    low = jnp.min(functools.reduce(jnp.minimum, peaks), axis=1, keepdims=True)
    low = jnp.broadcast_to(low, (AL, LANES))
    width = jnp.broadcast_to(high, (AL, LANES)) - low
    ways = 16
    for _ in range(6):
        width = width * (1.0 / ways)
        steps = jnp.zeros((AL, LANES), f32)
        for i in range(1, ways):
            bound = low + width * float(i)
            count = functools.reduce(
                jnp.add, [jnp.where(x >= bound, 1.0, 0.0) for x in xs]
            )
            count = jnp.sum(count, axis=1, keepdims=True)
            steps = steps + jnp.where(count >= float(T), 1.0, 0.0)
        low = low + width * steps
    above = functools.reduce(jnp.add, [jnp.maximum(x - low, 0.0) for x in xs])
    above = jnp.sum(above, axis=1, keepdims=True)
    marg_ref[...] = low + above * (1.0 / T)


def body(
    returns,
    prior,
    decay,
    seed_var,
    date_offsets,
    block_index,
    delta_sens,
    gamma_sens,
    positions,
    pattern,
):
    R, F = returns.shape
    S, I, A = lax.axis_size("scen"), lax.axis_size("inst"), lax.axis_size("acct")
    owners = I * A
    C, L, H = F // LANES, R // SUB, WIN - 1
    BW, instr = delta_sens.shape
    accts = positions.shape[0]
    AL = accts // (S * owners)
    AT = min(accts, 128)
    T = S * R // 40
    f32, bf16, i32 = jnp.float32, jnp.bfloat16, jnp.int32
    dma = pltpu.SemaphoreType.DMA
    acct_pnl, margin = pl.pallas_call(
        functools.partial(kernel, (S, I, A, T)),
        out_shape=(
            jax.ShapeDtypeStruct((AL, S * R), f32),
            jax.ShapeDtypeStruct((AL, LANES), f32),
        ),
        in_specs=[pl.BlockSpec(memory_space=pl.ANY)] * 10,
        out_specs=[pl.BlockSpec(memory_space=pltpu.VMEM)] * 2,
        scratch_shapes=[
            pltpu.VMEM((C, R, LANES), f32),
            pltpu.VMEM((H, F), f32),
            pltpu.VMEM((C, LANES), f32),
            pltpu.VMEM((C, LANES), f32),
            pltpu.VMEM((1, R), i32),
            pltpu.VMEM((1, instr), i32),
            pltpu.VMEM((2 * BW, instr), bf16),
            pltpu.VMEM((accts, instr), bf16),
            pltpu.VMEM(pattern.shape, i32),
            pltpu.VMEM((L, SUB, LANES), f32),
            pltpu.VMEM((L, C, SUB, LANES), f32),
            pltpu.VMEM((C, SUB, LANES), f32),
            pltpu.VMEM((S, C, LANES), f32),
            pltpu.VMEM((2 * H, C, LANES), f32),
            pltpu.VMEM((2 * H, C, LANES), f32),
            pltpu.VMEM((C, R, LANES), f32),
            pltpu.VMEM((C, accts, 2 * BW), f32),
            pltpu.VMEM((accts // AT, C, 2 * AT, 2 * BW), bf16),
            pltpu.VMEM((C, R, 2 * LANES), bf16),
            pltpu.VMEM((owners, S, AL, R), f32),
            pltpu.VMEM((owners - 1, S, AL, R), f32),
            pltpu.VMEM((S, AL, R), f32),
            pltpu.VMEM((S, AL, R), f32),
            dma((9,)),
            dma((C,)),
            dma((S,)),
            dma((S,)),
            dma,
            dma,
            dma((owners,)),
            dma((owners,)),
            dma((S,)),
            dma((S,)),
        ],
        compiler_params=pltpu.CompilerParams(
            collective_id=0, has_side_effects=True, vmem_limit_bytes=60 * 1024 * 1024
        ),
    )(
        returns,
        prior,
        decay.reshape(C, LANES),
        seed_var.reshape(C, LANES),
        date_offsets.reshape(1, R),
        block_index.reshape(1, instr),
        delta_sens,
        gamma_sens,
        positions,
        pattern,
    )
    return acct_pnl, margin[:, 0]


def solution(mesh):
    placed = (
        P(("group", "scen"), None),
        P("group", None),
        P(),
        P(),
        P("scen"),
        P(("group", "inst", "acct")),
        P(None, ("group", "inst", "acct")),
        P(None, ("group", "inst", "acct")),
        P("group", ("inst", "acct")),
        P("group", ("inst", "acct")),
    )
    return jax.shard_map(
        body,
        mesh=mesh,
        in_specs=placed,
        out_specs=(
            P(("group", "scen", "inst", "acct"), None),
            P(("group", "scen", "inst", "acct")),
        ),
        check_vma=False,
    )
```

```python
import functools

import jax
import jax.numpy as jnp
from jax import lax
from jax.experimental import pallas as pl
from jax.experimental.pallas import tpu as pltpu
from jax.sharding import PartitionSpec as P

WIN = 10
LANES = 128
SUB = 8
MESH = pl.DeviceIdType.MESH
NT = (((1,), (1,)), ((), ()))


def ipow(x, n):
    result = None
    while n:
        if n & 1:
            result = x if result is None else result * x
        n >>= 1
        if n:
            x = x * x
    return result


def kernel(
    sizes,
    ret_h, prior_h, dec_h, seed_h, off_h, bidx_h, delta_h, gamma_h, pos_h, pat_h,
    out_ref,
    pick, ret, prior, dec, seed, off, bidx, sens, pos, pat,
    offb, state, start, ends, tail_out, tail_in, moves, wacc, whl, fcat,
    part, rs_in, summ, fin,
    in_sem, ret_sem, end_ss, end_rs, tail_ss, tail_rs, rs_ss, rs_rs, fin_ss, fin_rs,
):
    S, I, A, T = sizes
    owners = I * A
    rank = lax.axis_index("scen")
    inst, acct = lax.axis_index("inst"), lax.axis_index("acct")
    me = inst * A + acct
    L, _, F = ret.shape
    C, R = F // LANES, L * SUB
    H = WIN - 1
    BW = delta_h.shape[0]
    accts, instr = pos.shape
    AL = accts // (S * owners)
    f32, bf16 = jnp.float32, jnp.bfloat16

    small = [
        pltpu.make_async_copy(src, dst, in_sem.at[n])
        for n, (src, dst) in enumerate(
            [(off_h, off), (dec_h, dec), (seed_h, seed), (prior_h, prior)]
        )
    ]
    late = [
        pltpu.make_async_copy(src, dst, in_sem.at[4 + n])
        for n, (src, dst) in enumerate(
            [
                (bidx_h, bidx),
                (pat_h, pat),
                (delta_h, sens.at[pl.ds(0, BW)]),
                (gamma_h, sens.at[pl.ds(BW, BW)]),
                (pos_h, pos),
            ]
        )
    ]
    cols = [
        pltpu.make_async_copy(
            ret_h.at[pl.ds(j * L, L), :], ret.at[:, j, :], ret_sem.at[j]
        )
        for j in range(SUB)
    ]
    for copy in small + cols + late:
        copy.start()

    def owner_id(d):
        who = lax.rem(me + d, owners)
        return {"inst": who // A, "acct": lax.rem(who, A)}

    barrier = pltpu.get_barrier_semaphore()
    for d in range(1, S):
        pl.semaphore_signal(
            barrier, inc=1, device_id={"scen": lax.rem(rank + d, S)}, device_id_type=MESH
        )
    for d in range(1, owners):
        pl.semaphore_signal(barrier, inc=1, device_id=owner_id(d), device_id_type=MESH)

    for copy in small:
        copy.wait()
    row = lax.broadcasted_iota(jnp.int32, (R, R), 0)
    day = lax.broadcasted_iota(jnp.int32, (R, R), 1)
    pick[...] = jnp.where((row % SUB) * L + row // SUB == day, 1.0, 0.0).astype(bf16)
    spread = jnp.broadcast_to(off[...].astype(f32), (LANES, R)).astype(bf16)
    offb[...] = lax.dot_general(pick[...], spread, NT, preferred_element_type=f32).reshape(
        L, SUB, LANES
    )

    keep_rows = 1.0 - dec[...]
    dec_c = [jnp.broadcast_to(dec[c : c + 1, :], (SUB, LANES)) for c in range(C)]
    keep_c = [1.0 - dec_c[c] for c in range(C)]
    for copy in cols:
        copy.wait()

    def scan(t, carry):
        new = []
        for c in range(C):
            x = ret[t, :, c * LANES : (c + 1) * LANES]
            v = keep_c[c] * carry[c] + dec_c[c] * x * x
            state[t, c] = v
            new.append(v)
        return tuple(new)

    zero = jnp.zeros((SUB, LANES), f32)
    last = lax.fori_loop(0, L, scan, (zero,) * C, unroll=4)

    sub = lax.broadcasted_iota(jnp.int32, (SUB, LANES), 0)
    for c in range(C):
        run = ipow(keep_c[c], L)
        x = last[c]
        for hop in (1, 2, 4):
            x = x + jnp.where(sub >= hop, run * pltpu.roll(x, hop, 0), 0.0)
            run = run * run
        ends[rank, c : c + 1, :] = x[SUB - 1 :, :]
        before = jnp.where(sub >= 1, pltpu.roll(x, 1, 0), 0.0)
        start[c] = before
        z = ipow(keep_c[c], L - H) * before
        for n in range(H):
            z = z * keep_c[c]
            v = state[L - H + n, c] + z
            tail_out[n, c : c + 1, :] = ret[L - H + n, SUB - 1 :, c * LANES : (c + 1) * LANES]
            tail_out[H + n, c : c + 1, :] = v[SUB - 1 :, :]

    pl.semaphore_wait(barrier, S - 1 + owners - 1)
    sends = []
    for d in range(1, S):
        sends.append(
            pltpu.make_async_remote_copy(
                src_ref=ends.at[rank],
                dst_ref=ends.at[rank],
                send_sem=end_ss.at[d],
                recv_sem=end_rs.at[d],
                device_id={"scen": lax.rem(rank + d, S)},
                device_id_type=MESH,
            )
        )
    sends.append(
        pltpu.make_async_remote_copy(
            src_ref=tail_out,
            dst_ref=tail_in,
            send_sem=tail_ss,
            recv_sem=tail_rs,
            device_id={"scen": lax.rem(rank + 1, S)},
            device_id_type=MESH,
        )
    )
    for copy in sends:
        copy.start()

    for copy in late:
        copy.wait()
    AT = min(accts, 128)
    CH = min(instr, 1024)
    blocks = pat.shape[0]
    PB = instr // blocks

    wacc[...] = jnp.zeros_like(wacc)

    def weigh(step, _):
        q, at = step // (accts // AT), lax.rem(step, accts // AT)
        rows = pl.ds(pl.multiple_of(at * AT, AT), AT)
        at_cols = pl.ds(pl.multiple_of(q * CH, CH), CH)
        ahead = lax.broadcasted_iota(jnp.int32, (blocks, CH), 1) + q * CH
        which = lax.broadcasted_iota(jnp.int32, (blocks, CH), 0) * PB
        widen = jnp.where((ahead >= which) & (ahead < which + PB), 1.0, 0.0).astype(bf16)
        holds = jnp.where(pat[:, rows] > 0, 1.0, 0.0).astype(bf16)
        mask = lax.dot_general(
            holds, widen, (((0,), (0,)), ((), ())), preferred_element_type=f32
        ).astype(bf16)
        held = pos[rows, at_cols] * mask
        own = bidx[:, at_cols]
        parts = [
            held * jnp.broadcast_to(jnp.where(own == b, 1.0, 0.0), (AT, CH)).astype(bf16)
            for b in range(C)
        ]
        got = lax.dot_general(
            jnp.concatenate(parts, axis=0), sens[:, at_cols], NT, preferred_element_type=f32
        )
        wacc[:, rows, :] += got.reshape(C, AT, 2 * BW)
        return 0

    lax.fori_loop(0, (instr // CH) * (accts // AT), weigh, 0)

    def split(step, _):
        c, at = step // (accts // AT), lax.rem(step, accts // AT)
        w = wacc[c, pl.ds(pl.multiple_of(at * AT, AT), AT), :]
        high = w.astype(bf16)
        whl[at, c, :AT, :] = high
        whl[at, c, AT:, :] = (w - high.astype(f32)).astype(bf16)
        return 0

    lax.fori_loop(0, C * (accts // AT), split, 0)

    for copy in sends:
        copy.wait()

    span = ipow(keep_rows, R)
    var = seed[...]
    entering = var
    entering_prev = var
    for n in range(S):
        entering = jnp.where(rank == n, var, entering)
        entering_prev = jnp.where(rank == n + 1, var, entering_prev)
        var = span * var + ends[n]
    root = jnp.sqrt(var)

    power = ipow(keep_rows, R - H)
    lead = []
    for n in range(H):
        power = power * keep_rows
        lead.append(
            tail_in[n] * (root * lax.rsqrt(tail_in[H + n] + power * entering_prev))
        )

    root_c, z0, heads = [], [], [[] for _ in range(C)]
    for c in range(C):
        root_b = jnp.broadcast_to(root[c : c + 1, :], (SUB, LANES))
        enter_b = jnp.broadcast_to(entering[c : c + 1, :], (SUB, LANES))
        run = ipow(keep_c[c], L)
        run_pow = jnp.ones((SUB, LANES), f32)
        for j in range(1, SUB):
            run_pow = jnp.where(sub >= j, run_pow * run, run_pow)
        z = start[c] + run_pow * enter_b
        root_c.append(root_b)
        z0.append(z)
        z = z * ipow(keep_c[c], L - H)
        for n in range(H):
            z = z * keep_c[c]
            t = L - H + n
            x = ret[t, :, c * LANES : (c + 1) * LANES]
            e = x * (root_b * lax.rsqrt(state[t, c] + z))
            first = jnp.where(
                rank == 0,
                prior[n : n + 1, c * LANES : (c + 1) * LANES],
                lead[n][c : c + 1, :],
            )
            heads[c].append(
                jnp.where(sub == 0, jnp.broadcast_to(first, (SUB, LANES)), pltpu.roll(e, 1, 0))
            )

    G, PAIR = 8, 2

    def window(group, block, carry):
        t0 = block * G
        new = []
        offs = [offb[t0 + i] for i in range(G)]
        for c, (z, e) in zip(group, carry):
            e = list(e)
            for i in range(G):
                z = z * keep_c[c]
                x = ret[t0 + i, :, c * LANES : (c + 1) * LANES]
                e.append(x * (root_c[c] * lax.rsqrt(state[t0 + i, c] + z)))
            new.append((z, tuple(e[G:])))
            two = {i: e[i] + e[i - 1] for i in range(3, G + H)}
            four = {i: two[i] + two[i - 2] for i in range(5, G + H)}
            for i in range(G):
                p = i + H
                total = four[p] + four[p - 4]
                total = total + jnp.where(offs[i] < 1.5, e[p - 8], 0.0)
                total = total + jnp.where(offs[i] < 0.5, e[p - 9], 0.0)
                moves[c, t0 + i] = total
        return tuple(new)

    for g in range(0, C, PAIR):
        group = tuple(range(g, min(g + PAIR, C)))
        lax.fori_loop(
            0, L // G, functools.partial(window, group), tuple((z0[c], tuple(heads[c])) for c in group)
        )

    for c in range(C):
        m = moves[c].reshape(R, LANES)
        fcat[c, :, :LANES] = m.astype(bf16)
        fcat[c, :, LANES:] = (0.5 * m * m).astype(bf16)

    per = AT // AL

    def combine(at, _):
        both = jnp.zeros((2 * AT, R), f32)
        for c in range(C):
            both = both + lax.dot_general(
                whl[at, c], fcat[c], NT, preferred_element_type=f32
            )
        total = both[:AT] + both[AT:]
        for i in range(per):
            part[i % owners, at * (per // owners) + i // owners] = total[i * AL : (i + 1) * AL]
        return 0

    lax.fori_loop(0, accts // AT, combine, 0)

    hops = []
    for d in range(1, owners):
        hops.append(
            pltpu.make_async_remote_copy(
                src_ref=part.at[lax.rem(me + d, owners)],
                dst_ref=rs_in.at[d - 1],
                send_sem=rs_ss.at[d],
                recv_sem=rs_rs.at[d],
                device_id=owner_id(d),
                device_id_type=MESH,
            )
        )
    for copy in hops:
        copy.start()
    for copy in hops:
        copy.wait()
    total = part[me]
    for d in range(1, owners):
        total = total + rs_in[d - 1]
    rows = total.reshape(S * AL, R)
    pieces = []
    for _ in range(3):
        piece = rows.astype(bf16)
        pieces.append(piece)
        rows = rows - piece.astype(f32)
    first, second, third = [
        jnp.dot(piece, pick[...], preferred_element_type=f32) for piece in pieces
    ]
    summ[...] = ((first + second) + third).reshape(S, AL, R)

    outs = []
    for d in range(1, S):
        to = lax.rem(rank + d, S)
        outs.append(
            pltpu.make_async_remote_copy(
                src_ref=summ.at[to],
                dst_ref=fin.at[rank],
                send_sem=fin_ss.at[d],
                recv_sem=fin_rs.at[d],
                device_id={"scen": to},
                device_id_type=MESH,
            )
        )
    for copy in outs:
        copy.start()
    fin[rank] = summ[rank]
    for copy in outs:
        copy.wait()
    out_ref[...] = fin[...]


def tail_kernel(T, fin, out_ref, marg_ref):
    S, AL, R = fin.shape
    f32 = jnp.float32
    xs = []
    for k in range(S):
        y = fin[k]
        out_ref[:, k * R : (k + 1) * R] = y
        xs.extend(-y[:, i * LANES : (i + 1) * LANES] for i in range(R // LANES))

    groups = -(-T // LANES)
    each = len(xs) // groups
    peaks = []
    for g in range(groups):
        mine = xs[g * each : (g + 1) * each] if g < groups - 1 else xs[g * each :]
        peaks.append(functools.reduce(jnp.maximum, mine))
    high = jnp.max(functools.reduce(jnp.maximum, peaks), axis=1, keepdims=True)
    low = jnp.min(functools.reduce(jnp.minimum, peaks), axis=1, keepdims=True)
    low = jnp.broadcast_to(low, (AL, LANES))
    width = jnp.broadcast_to(high, (AL, LANES)) - low
    ways = 16
    for _ in range(6):
        width = width * (1.0 / ways)
        steps = jnp.zeros((AL, LANES), f32)
        for i in range(1, ways):
            bound = low + width * float(i)
            count = functools.reduce(
                jnp.add, [jnp.where(x >= bound, 1.0, 0.0) for x in xs]
            )
            count = jnp.sum(count, axis=1, keepdims=True)
            steps = steps + jnp.where(count >= float(T), 1.0, 0.0)
        low = low + width * steps
    above = functools.reduce(jnp.add, [jnp.maximum(x - low, 0.0) for x in xs])
    above = jnp.sum(above, axis=1, keepdims=True)
    short = low + above * (1.0 / T)
    lane = lax.broadcasted_iota(jnp.int32, (AL, LANES), 1)
    mine = lane == lax.broadcasted_iota(jnp.int32, (AL, LANES), 0)
    marg_ref[...] = jnp.sum(jnp.where(mine, short, 0.0), axis=0)[:AL]


def body(
    returns,
    prior,
    decay,
    seed_var,
    date_offsets,
    block_index,
    delta_sens,
    gamma_sens,
    positions,
    pattern,
):
    R, F = returns.shape
    S, I, A = lax.axis_size("scen"), lax.axis_size("inst"), lax.axis_size("acct")
    owners = I * A
    C, L, H = F // LANES, R // SUB, WIN - 1
    BW, instr = delta_sens.shape
    accts = positions.shape[0]
    AL = accts // (S * owners)
    AT = min(accts, 128)
    T = S * R // 40
    f32, bf16, i32 = jnp.float32, jnp.bfloat16, jnp.int32
    dma = pltpu.SemaphoreType.DMA
    joined = pl.pallas_call(
        functools.partial(kernel, (S, I, A, T)),
        out_shape=jax.ShapeDtypeStruct((S, AL, R), f32),
        in_specs=[pl.BlockSpec(memory_space=pl.ANY)] * 10,
        out_specs=pl.BlockSpec(memory_space=pltpu.VMEM),
        scratch_shapes=[
            pltpu.VMEM((R, R), bf16),
            pltpu.VMEM((L, SUB, F), f32),
            pltpu.VMEM((H, F), f32),
            pltpu.VMEM((C, LANES), f32),
            pltpu.VMEM((C, LANES), f32),
            pltpu.VMEM((1, R), i32),
            pltpu.VMEM((1, instr), i32),
            pltpu.VMEM((2 * BW, instr), bf16),
            pltpu.VMEM((accts, instr), bf16),
            pltpu.VMEM(pattern.shape[::-1], i32),
            pltpu.VMEM((L, SUB, LANES), f32),
            pltpu.VMEM((L, C, SUB, LANES), f32),
            pltpu.VMEM((C, SUB, LANES), f32),
            pltpu.VMEM((S, C, LANES), f32),
            pltpu.VMEM((2 * H, C, LANES), f32),
            pltpu.VMEM((2 * H, C, LANES), f32),
            pltpu.VMEM((C, L, SUB, LANES), f32),
            pltpu.VMEM((C, accts, 2 * BW), f32),
            pltpu.VMEM((accts // AT, C, 2 * AT, 2 * BW), bf16),
            pltpu.VMEM((C, R, 2 * LANES), bf16),
            pltpu.VMEM((owners, S, AL, R), f32),
            pltpu.VMEM((owners - 1, S, AL, R), f32),
            pltpu.VMEM((S, AL, R), f32),
            pltpu.VMEM((S, AL, R), f32),
            dma((9,)),
            dma((SUB,)),
            dma((S,)),
            dma((S,)),
            dma,
            dma,
            dma((owners,)),
            dma((owners,)),
            dma((S,)),
            dma((S,)),
        ],
        compiler_params=pltpu.CompilerParams(
            collective_id=0, has_side_effects=True, vmem_limit_bytes=60 * 1024 * 1024
        ),
    )(
        returns,
        prior,
        decay.reshape(C, LANES),
        seed_var.reshape(C, LANES),
        date_offsets.reshape(1, R),
        block_index.reshape(1, instr),
        delta_sens,
        gamma_sens,
        positions,
        pattern.T,
    )
    return pl.pallas_call(
        functools.partial(tail_kernel, T),
        out_shape=(
            jax.ShapeDtypeStruct((AL, S * R), f32),
            jax.ShapeDtypeStruct((AL,), f32),
        ),
        in_specs=[pl.BlockSpec(memory_space=pltpu.VMEM)],
        out_specs=[pl.BlockSpec(memory_space=pltpu.VMEM)] * 2,
    )(joined)


def solution(mesh):
    placed = (
        P(("group", "scen"), None),
        P("group", None),
        P(),
        P(),
        P("scen"),
        P(("group", "inst", "acct")),
        P(None, ("group", "inst", "acct")),
        P(None, ("group", "inst", "acct")),
        P("group", ("inst", "acct")),
        P("group", ("inst", "acct")),
    )
    return jax.shard_map(
        body,
        mesh=mesh,
        in_specs=placed,
        out_specs=(
            P(("group", "scen", "inst", "acct"), None),
            P(("group", "scen", "inst", "acct")),
        ),
        check_vma=False,
    )
```

```python
import functools

import jax
import jax.numpy as jnp
from jax import lax
from jax.experimental import pallas as pl
from jax.experimental.pallas import tpu as pltpu
from jax.sharding import PartitionSpec as P

WIN = 10
HALVES = 2
LANES = 128
SUB = 8
MESH = pl.DeviceIdType.MESH
NT = (((1,), (1,)), ((), ()))


def ipow(x, n):
    result = None
    while n:
        if n & 1:
            result = x if result is None else result * x
        n >>= 1
        if n:
            x = x * x
    return result


def kernel(
    sizes,
    ret_h, prior_h, dec_h, seed_h, off_h, bidx_h, delta_h, gamma_h, pos_h, pat_h,
    out_ref,
    pick, ret, prior, dec, seed, off, bidx, sens, pos, pat,
    offb, state, start, ends, tail_out, tail_in, moves, wacc, whl, fcat,
    part, rs_in, summ, fin,
    in_sem, ret_sem, end_ss, end_rs, tail_ss, tail_rs, rs_ss, rs_rs, fin_ss, fin_rs,
):
    S, I, A, T = sizes
    owners = I * A
    rank = lax.axis_index("scen")
    inst, acct = lax.axis_index("inst"), lax.axis_index("acct")
    me = inst * A + acct
    L, _, F = ret.shape
    C, R = F // LANES, L * SUB
    H = WIN - 1
    BW = delta_h.shape[0]
    accts, instr = pos.shape
    AL = accts // (S * owners)
    f32, bf16 = jnp.float32, jnp.bfloat16

    small = [
        pltpu.make_async_copy(src, dst, in_sem.at[n])
        for n, (src, dst) in enumerate(
            [(off_h, off), (dec_h, dec), (seed_h, seed), (prior_h, prior)]
        )
    ]
    late = [
        pltpu.make_async_copy(src, dst, in_sem.at[4 + n])
        for n, (src, dst) in enumerate(
            [
                (bidx_h, bidx),
                (pat_h, pat),
                (delta_h, sens.at[pl.ds(0, BW)]),
                (gamma_h, sens.at[pl.ds(BW, BW)]),
                (pos_h, pos),
            ]
        )
    ]
    cols = [
        pltpu.make_async_copy(
            ret_h.at[pl.ds(j * L, L), :], ret.at[:, j, :], ret_sem.at[j]
        )
        for j in range(SUB)
    ]
    for copy in small + cols + late:
        copy.start()

    def owner_id(d):
        who = lax.rem(me + d, owners)
        return {"inst": who // A, "acct": lax.rem(who, A)}

    barrier = pltpu.get_barrier_semaphore()
    for d in range(1, S):
        pl.semaphore_signal(
            barrier, inc=1, device_id={"scen": lax.rem(rank + d, S)}, device_id_type=MESH
        )
    for d in range(1, owners):
        pl.semaphore_signal(barrier, inc=1, device_id=owner_id(d), device_id_type=MESH)

    for copy in small:
        copy.wait()
    row = lax.broadcasted_iota(jnp.int32, (R, R), 0)
    day = lax.broadcasted_iota(jnp.int32, (R, R), 1)
    pick[...] = jnp.where((row % SUB) * L + row // SUB == day, 1.0, 0.0).astype(bf16)
    spread = jnp.broadcast_to(off[...].astype(f32), (LANES, R)).astype(bf16)
    offb[...] = lax.dot_general(pick[...], spread, NT, preferred_element_type=f32).reshape(
        L, SUB, LANES
    )

    keep_rows = 1.0 - dec[...]
    dec_c = [jnp.broadcast_to(dec[c : c + 1, :], (SUB, LANES)) for c in range(C)]
    keep_c = [1.0 - dec_c[c] for c in range(C)]
    for copy in cols:
        copy.wait()

    def scan(t, carry):
        new = []
        for c in range(C):
            x = ret[t, :, c * LANES : (c + 1) * LANES]
            v = keep_c[c] * carry[c] + dec_c[c] * x * x
            state[t, c] = v
            new.append(v)
        return tuple(new)

    zero = jnp.zeros((SUB, LANES), f32)
    last = lax.fori_loop(0, L, scan, (zero,) * C, unroll=4)

    sub = lax.broadcasted_iota(jnp.int32, (SUB, LANES), 0)
    for c in range(C):
        run = ipow(keep_c[c], L)
        x = last[c]
        for hop in (1, 2, 4):
            x = x + jnp.where(sub >= hop, run * pltpu.roll(x, hop, 0), 0.0)
            run = run * run
        ends[rank, c : c + 1, :] = x[SUB - 1 :, :]
        before = jnp.where(sub >= 1, pltpu.roll(x, 1, 0), 0.0)
        start[c] = before
        z = ipow(keep_c[c], L - H) * before
        for n in range(H):
            z = z * keep_c[c]
            v = state[L - H + n, c] + z
            tail_out[n, c : c + 1, :] = ret[L - H + n, SUB - 1 :, c * LANES : (c + 1) * LANES]
            tail_out[H + n, c : c + 1, :] = v[SUB - 1 :, :]

    pl.semaphore_wait(barrier, S - 1 + owners - 1)
    sends = []
    for d in range(1, S):
        sends.append(
            pltpu.make_async_remote_copy(
                src_ref=ends.at[rank],
                dst_ref=ends.at[rank],
                send_sem=end_ss.at[d],
                recv_sem=end_rs.at[d],
                device_id={"scen": lax.rem(rank + d, S)},
                device_id_type=MESH,
            )
        )
    sends.append(
        pltpu.make_async_remote_copy(
            src_ref=tail_out,
            dst_ref=tail_in,
            send_sem=tail_ss,
            recv_sem=tail_rs,
            device_id={"scen": lax.rem(rank + 1, S)},
            device_id_type=MESH,
        )
    )
    for copy in sends:
        copy.start()

    for copy in late:
        copy.wait()
    AT = min(accts, 128)
    CH = min(instr, 1024)
    blocks = pat.shape[0]
    PB = instr // blocks

    wacc[...] = jnp.zeros_like(wacc)

    def weigh(step, _):
        q, at = step // (accts // AT), lax.rem(step, accts // AT)
        rows = pl.ds(pl.multiple_of(at * AT, AT), AT)
        at_cols = pl.ds(pl.multiple_of(q * CH, CH), CH)
        ahead = lax.broadcasted_iota(jnp.int32, (blocks, CH), 1) + q * CH
        which = lax.broadcasted_iota(jnp.int32, (blocks, CH), 0) * PB
        widen = jnp.where((ahead >= which) & (ahead < which + PB), 1.0, 0.0).astype(bf16)
        holds = jnp.where(pat[:, rows] > 0, 1.0, 0.0).astype(bf16)
        mask = lax.dot_general(
            holds, widen, (((0,), (0,)), ((), ())), preferred_element_type=f32
        ).astype(bf16)
        held = pos[rows, at_cols] * mask
        own = bidx[:, at_cols]
        parts = [
            held * jnp.broadcast_to(jnp.where(own == b, 1.0, 0.0), (AT, CH)).astype(bf16)
            for b in range(C)
        ]
        got = lax.dot_general(
            jnp.concatenate(parts, axis=0), sens[:, at_cols], NT, preferred_element_type=f32
        )
        wacc[:, rows, :] += got.reshape(C, AT, 2 * BW)
        return 0

    lax.fori_loop(0, (instr // CH) * (accts // AT), weigh, 0)

    def split(step, _):
        c, at = step // (accts // AT), lax.rem(step, accts // AT)
        w = wacc[c, pl.ds(pl.multiple_of(at * AT, AT), AT), :]
        high = w.astype(bf16)
        whl[at, c, :AT, :] = high
        whl[at, c, AT:, :] = (w - high.astype(f32)).astype(bf16)
        return 0

    lax.fori_loop(0, C * (accts // AT), split, 0)

    for copy in sends:
        copy.wait()

    span = ipow(keep_rows, R)
    var = seed[...]
    entering = var
    entering_prev = var
    for n in range(S):
        entering = jnp.where(rank == n, var, entering)
        entering_prev = jnp.where(rank == n + 1, var, entering_prev)
        var = span * var + ends[n]
    root = jnp.sqrt(var)

    power = ipow(keep_rows, R - H)
    lead = []
    for n in range(H):
        power = power * keep_rows
        lead.append(
            tail_in[n] * (root * lax.rsqrt(tail_in[H + n] + power * entering_prev))
        )

    root_c, z0, heads = [], [], [[] for _ in range(C)]
    for c in range(C):
        root_b = jnp.broadcast_to(root[c : c + 1, :], (SUB, LANES))
        enter_b = jnp.broadcast_to(entering[c : c + 1, :], (SUB, LANES))
        run = ipow(keep_c[c], L)
        run_pow = jnp.ones((SUB, LANES), f32)
        for j in range(1, SUB):
            run_pow = jnp.where(sub >= j, run_pow * run, run_pow)
        z = start[c] + run_pow * enter_b
        root_c.append(root_b)
        z0.append(z)
        z = z * ipow(keep_c[c], L - H)
        for n in range(H):
            z = z * keep_c[c]
            t = L - H + n
            x = ret[t, :, c * LANES : (c + 1) * LANES]
            e = x * (root_b * lax.rsqrt(state[t, c] + z))
            first = jnp.where(
                rank == 0,
                prior[n : n + 1, c * LANES : (c + 1) * LANES],
                lead[n][c : c + 1, :],
            )
            heads[c].append(
                jnp.where(sub == 0, jnp.broadcast_to(first, (SUB, LANES)), pltpu.roll(e, 1, 0))
            )

    G, PAIR = 8, 2

    def window(group, block, carry):
        t0 = block * G
        new = []
        offs = [offb[t0 + i] for i in range(G)]
        for c, (z, e) in zip(group, carry):
            e = list(e)
            for i in range(G):
                z = z * keep_c[c]
                x = ret[t0 + i, :, c * LANES : (c + 1) * LANES]
                e.append(x * (root_c[c] * lax.rsqrt(state[t0 + i, c] + z)))
            new.append((z, tuple(e[G:])))
            two = {i: e[i] + e[i - 1] for i in range(3, G + H)}
            four = {i: two[i] + two[i - 2] for i in range(5, G + H)}
            for i in range(G):
                p = i + H
                total = four[p] + four[p - 4]
                total = total + jnp.where(offs[i] < 1.5, e[p - 8], 0.0)
                total = total + jnp.where(offs[i] < 0.5, e[p - 9], 0.0)
                moves[c, t0 + i] = total
        return tuple(new)

    per = AT // AL
    RH = R // HALVES
    ahead_of = [(z0[c], tuple(heads[c])) for c in range(C)]
    hops = []
    for half in range(HALVES):
        first, past = half * (L // G) // HALVES, (half + 1) * (L // G) // HALVES
        for g in range(0, C, PAIR):
            group = tuple(range(g, min(g + PAIR, C)))
            ahead_of[g : g + PAIR] = lax.fori_loop(
                first, past, functools.partial(window, group), tuple(ahead_of[g : g + PAIR])
            )
        for c in range(C):
            m = moves[c, half * (L // HALVES) : (half + 1) * (L // HALVES)].reshape(RH, LANES)
            fcat[half, c, :, :LANES] = m.astype(bf16)
            fcat[half, c, :, LANES:] = (0.5 * m * m).astype(bf16)

        def combine(at, _, half=half):
            both = jnp.zeros((2 * AT, RH), f32)
            for c in range(C):
                both = both + lax.dot_general(
                    whl[at, c], fcat[half, c], NT, preferred_element_type=f32
                )
            total = both[:AT] + both[AT:]
            for i in range(per):
                part[half, i % owners, at * (per // owners) + i // owners] = total[
                    i * AL : (i + 1) * AL
                ]
            return 0

        lax.fori_loop(0, accts // AT, combine, 0)
        hops.append(
            [
                pltpu.make_async_remote_copy(
                    src_ref=part.at[half, lax.rem(me + d, owners)],
                    dst_ref=rs_in.at[half, d - 1],
                    send_sem=rs_ss.at[half, d],
                    recv_sem=rs_rs.at[half, d],
                    device_id=owner_id(d),
                    device_id_type=MESH,
                )
                for d in range(1, owners)
            ]
        )
        for copy in hops[half]:
            copy.start()

    outs = []
    for half in range(HALVES):
        for copy in hops[half]:
            copy.wait_recv()
        total = part[half, me]
        for d in range(1, owners):
            total = total + rs_in[half, d - 1]
        summ[half] = total
        outs.append(
            [
                pltpu.make_async_remote_copy(
                    src_ref=summ.at[half, lax.rem(rank + d, S)],
                    dst_ref=fin.at[half, rank],
                    send_sem=fin_ss.at[half, d],
                    recv_sem=fin_rs.at[half, d],
                    device_id={"scen": lax.rem(rank + d, S)},
                    device_id_type=MESH,
                )
                for d in range(1, S)
            ]
        )
        for copy in outs[half]:
            copy.start()
        fin[half, rank] = summ[half, rank]
    dated = jnp.zeros((S * AL, R), f32)
    for half in range(HALVES):
        for copy in outs[half]:
            copy.wait()
        rows = fin[half].reshape(S * AL, RH)
        pieces = []
        for _ in range(3):
            piece = rows.astype(bf16)
            pieces.append(piece)
            rows = rows - piece.astype(f32)
        days = pick[half * RH : (half + 1) * RH, :]
        one, two, three = [
            jnp.dot(piece, days, preferred_element_type=f32) for piece in pieces
        ]
        dated = dated + ((one + two) + three)
    out_ref[...] = dated.reshape(S, AL, R)
    for copies in hops:
        for copy in copies:
            copy.wait_send()


def tail_kernel(T, fin, out_ref, marg_ref):
    S, AL, R = fin.shape
    f32 = jnp.float32
    xs = []
    for k in range(S):
        y = fin[k]
        out_ref[:, k * R : (k + 1) * R] = y
        xs.extend(-y[:, i * LANES : (i + 1) * LANES] for i in range(R // LANES))

    groups = -(-T // LANES)
    each = len(xs) // groups
    peaks = []
    for g in range(groups):
        mine = xs[g * each : (g + 1) * each] if g < groups - 1 else xs[g * each :]
        peaks.append(functools.reduce(jnp.maximum, mine))
    high = jnp.max(functools.reduce(jnp.maximum, peaks), axis=1, keepdims=True)
    low = jnp.min(functools.reduce(jnp.minimum, peaks), axis=1, keepdims=True)
    low = jnp.broadcast_to(low, (AL, LANES))
    width = jnp.broadcast_to(high, (AL, LANES)) - low
    ways = 16
    for _ in range(6):
        width = width * (1.0 / ways)
        steps = jnp.zeros((AL, LANES), f32)
        for i in range(1, ways):
            bound = low + width * float(i)
            count = functools.reduce(
                jnp.add, [jnp.where(x >= bound, 1.0, 0.0) for x in xs]
            )
            count = jnp.sum(count, axis=1, keepdims=True)
            steps = steps + jnp.where(count >= float(T), 1.0, 0.0)
        low = low + width * steps
    above = functools.reduce(jnp.add, [jnp.maximum(x - low, 0.0) for x in xs])
    above = jnp.sum(above, axis=1, keepdims=True)
    short = low + above * (1.0 / T)
    lane = lax.broadcasted_iota(jnp.int32, (AL, LANES), 1)
    mine = lane == lax.broadcasted_iota(jnp.int32, (AL, LANES), 0)
    marg_ref[...] = jnp.sum(jnp.where(mine, short, 0.0), axis=0)[:AL]


def body(
    returns,
    prior,
    decay,
    seed_var,
    date_offsets,
    block_index,
    delta_sens,
    gamma_sens,
    positions,
    pattern,
):
    R, F = returns.shape
    S, I, A = lax.axis_size("scen"), lax.axis_size("inst"), lax.axis_size("acct")
    owners = I * A
    C, L, H = F // LANES, R // SUB, WIN - 1
    BW, instr = delta_sens.shape
    accts = positions.shape[0]
    AL = accts // (S * owners)
    AT = min(accts, 128)
    T = S * R // 40
    f32, bf16, i32 = jnp.float32, jnp.bfloat16, jnp.int32
    dma = pltpu.SemaphoreType.DMA
    joined = pl.pallas_call(
        functools.partial(kernel, (S, I, A, T)),
        out_shape=jax.ShapeDtypeStruct((S, AL, R), f32),
        in_specs=[pl.BlockSpec(memory_space=pl.ANY)] * 10,
        out_specs=pl.BlockSpec(memory_space=pltpu.VMEM),
        scratch_shapes=[
            pltpu.VMEM((R, R), bf16),
            pltpu.VMEM((L, SUB, F), f32),
            pltpu.VMEM((H, F), f32),
            pltpu.VMEM((C, LANES), f32),
            pltpu.VMEM((C, LANES), f32),
            pltpu.VMEM((1, R), i32),
            pltpu.VMEM((1, instr), i32),
            pltpu.VMEM((2 * BW, instr), bf16),
            pltpu.VMEM((accts, instr), bf16),
            pltpu.VMEM(pattern.shape[::-1], i32),
            pltpu.VMEM((L, SUB, LANES), f32),
            pltpu.VMEM((L, C, SUB, LANES), f32),
            pltpu.VMEM((C, SUB, LANES), f32),
            pltpu.VMEM((S, C, LANES), f32),
            pltpu.VMEM((2 * H, C, LANES), f32),
            pltpu.VMEM((2 * H, C, LANES), f32),
            pltpu.VMEM((C, L, SUB, LANES), f32),
            pltpu.VMEM((C, accts, 2 * BW), f32),
            pltpu.VMEM((accts // AT, C, 2 * AT, 2 * BW), bf16),
            pltpu.VMEM((HALVES, C, R // HALVES, 2 * LANES), bf16),
            pltpu.VMEM((HALVES, owners, S, AL, R // HALVES), f32),
            pltpu.VMEM((HALVES, owners - 1, S, AL, R // HALVES), f32),
            pltpu.VMEM((HALVES, S, AL, R // HALVES), f32),
            pltpu.VMEM((HALVES, S, AL, R // HALVES), f32),
            dma((9,)),
            dma((SUB,)),
            dma((S,)),
            dma((S,)),
            dma,
            dma,
            dma((HALVES, owners)),
            dma((HALVES, owners)),
            dma((HALVES, S)),
            dma((HALVES, S)),
        ],
        compiler_params=pltpu.CompilerParams(
            collective_id=0, has_side_effects=True, vmem_limit_bytes=60 * 1024 * 1024
        ),
    )(
        returns,
        prior,
        decay.reshape(C, LANES),
        seed_var.reshape(C, LANES),
        date_offsets.reshape(1, R),
        block_index.reshape(1, instr),
        delta_sens,
        gamma_sens,
        positions,
        pattern.T,
    )
    return pl.pallas_call(
        functools.partial(tail_kernel, T),
        out_shape=(
            jax.ShapeDtypeStruct((AL, S * R), f32),
            jax.ShapeDtypeStruct((AL,), f32),
        ),
        in_specs=[pl.BlockSpec(memory_space=pltpu.VMEM)],
        out_specs=[pl.BlockSpec(memory_space=pltpu.VMEM)] * 2,
    )(joined)


def solution(mesh):
    placed = (
        P(("group", "scen"), None),
        P("group", None),
        P(),
        P(),
        P("scen"),
        P(("group", "inst", "acct")),
        P(None, ("group", "inst", "acct")),
        P(None, ("group", "inst", "acct")),
        P("group", ("inst", "acct")),
        P("group", ("inst", "acct")),
    )
    return jax.shard_map(
        body,
        mesh=mesh,
        in_specs=placed,
        out_specs=(
            P(("group", "scen", "inst", "acct"), None),
            P(("group", "scen", "inst", "acct")),
        ),
        check_vma=False,
    )
```
